1024 devices in a mesh: row: 8 (over z_hi, core), col: 128 (over x, z_lo, y).
Axes of the slice: x: 8, y: 8, z: 8 (z_hi: 4, z_lo: 2; z = z_hi * 2 + z_lo), core: 2. Of those that a mesh axis runs over, the one named last changes fastest.
Arguments:
- vectors: float32 [16, 16, 1024, 256], P(None, 'row', 'col'), may hold values from -6 to 6
- leaf_order: int32 [16, 1024, 256], P('row', 'col'), may hold values from 0 to 255, each once within a row
- offsets: float32 [3, 16, 1024, 256], P(None, 'row', 'col'), may hold values from 0 to 1
- near_mask: int32 [9, 16, 1024], P(None, 'row', 'col'), may hold values 0 or 1
- far_mask: int32 [16, 16, 1024], P(None, 'row', 'col'), may hold values 0 or 1
- basis: float32 [16, 1024, 64, 256], P('row', 'col'), may hold values from -0.375 to 0.375
- transfer: float32 [16, 1024, 64, 64], P('row', 'col'), may hold values from -0.75 to 0.75
- coupling: float32 [16, 64, 64], replicated, may hold values from -0.25 to 0.25
- top_coupling: float32 [16, 64, 64], replicated, may hold values from -0.005859375 to 0.005859375
- cluster_owner: int32 [8, 128], P('row', 'col'), may hold values from 0 to 15
Outputs:
- product: float32 [16, 16, 1024, 256], P(None, 'row', 'col')
The draws below stay inside these ranges and needn't reach their ends.
Inputs may be any that keep to these rules, and one draw needn't show every extreme that they name: `leaf_order`: each leaf's entries are a permutation of 0 to 255.
All inputs are finite; a program needn't handle non-finite values. No bound on the sum of `near_mask` or of `far_mask` on one device may be relied on, other than what follows from the above.
Results may differ from the reference program's by a relative error of at most 0.0003.
Values sent between devices are 32-bit elements; how exact they have to be, the bound alone decides.
A program may use at most 32 MiB of HBM per device.

```python
import math
import jax
import jax.numpy as jnp
from jax import lax

LEAF = 256
RANK = 64
RHS = 16
LR = 2
LC = 8
TOPN = 16
LEAFR = 16
LEAFC = 1024
N_ROW = 8
N_COL = 128


def with_ends(drawn, stream_key, least, high):
    shape = drawn.shape
    spot = [jax.random.randint(jax.random.fold_in(stream_key, axis), (), 0, shape[axis]) for axis in range(len(shape))]
    drawn = drawn.at[tuple(spot)].set(least)
    longest = shape.index(max(shape))
    spot[longest] = (spot[longest] + 1) % shape[longest]
    return drawn.at[tuple(spot)].set(high)


def block_scale(stream_key, dims, cuts, least, high):
    factor_of = 1.0
    for axis_at, parts in cuts:
        draws = jax.random.uniform(jax.random.fold_in(jax.random.fold_in(stream_key, 6), axis_at), (parts,), jnp.float32, least / len(cuts), high / len(cuts))
        factor_of = factor_of * jnp.repeat(jnp.exp(draws), dims[axis_at] // parts).reshape((-1,) + (1,) * (len(dims) - 1 - axis_at))
    return factor_of


def noise(stream_key, shape, width, most, cuts=(), kind=jnp.bfloat16):
    values = width * jax.random.normal(stream_key, shape, jnp.float32)
    if cuts:
        values = values * block_scale(stream_key, shape, cuts, -0.22, 0.18)
    return jnp.clip(values, -most, most).astype(kind)


def setup_inputs(seed: int = 0) -> dict:
    key_of = jax.random.split(jax.random.key(seed), 11)
    vectors = noise(key_of[0], (RHS, LEAFR, LEAFC, LEAF), 1.0, 6.0, ((1, 8), (2, 128)), jnp.float32)
    leaf_order = jax.vmap(lambda own: jax.random.permutation(own, LEAF))(jax.random.split(key_of[1], LEAFR * LEAFC)).reshape((LEAFR, LEAFC, LEAF)).astype(jnp.int32)
    offsets = jnp.clip(1.0 * jax.random.uniform(key_of[2], (3, LEAFR, LEAFC, LEAF), jnp.float32) ** block_scale(key_of[2], (3, LEAFR, LEAFC, LEAF), ((1, 8), (2, 128)), -0.2, 0.2), 0.0, 1.0)
    near_mask = with_ends((jax.random.randint(key_of[3], (9, LEAFR, LEAFC), 0, 4) < 3).astype(jnp.int32), jax.random.fold_in(key_of[3], 1), 0, 1)
    far_mask = with_ends((jax.random.randint(key_of[4], (16, LEAFR, LEAFC), 0, 2) < 1).astype(jnp.int32), jax.random.fold_in(key_of[4], 1), 0, 1)
    basis = noise(key_of[5], (LEAFR, LEAFC, RANK, LEAF), LEAF ** -0.5, 0.375, ((0, 8), (1, 128)), jnp.float32)
    transfer = noise(key_of[6], (LEAFR, LEAFC, RANK, RANK), RANK ** -0.5, 0.75, ((0, 8), (1, 128)), jnp.float32)
    coupling = noise(key_of[7], (16, RANK, RANK), (RANK * 8) ** -0.5, 0.25, (), jnp.float32)
    top_coupling = noise(key_of[8], (TOPN, RANK, RANK), (RANK * LR * LC * N_ROW * N_COL) ** -0.5, 0.005859375, (), jnp.float32)
    cluster_owner = with_ends(jax.random.randint(key_of[9], (N_ROW, N_COL), 0, TOPN), jax.random.fold_in(key_of[9], 1), 0, TOPN - 1).astype(jnp.int32)
    return dict(vectors=vectors, leaf_order=leaf_order, offsets=offsets, near_mask=near_mask, far_mask=far_mask, basis=basis, transfer=transfer, coupling=coupling, top_coupling=top_coupling, cluster_owner=cluster_owner)


softening = 0.01

def far_offsets():
    found = []
    for down_step in range(-2, 3):
        for right_step in range(-2, 3):
            if max(abs(down_step), abs(right_step)) == 2:
                found.append((down_step, right_step))
    return found

def kernel_block(target, source):
    square = jnp.zeros(target.shape[1:] + (source.shape[-1],), jnp.float32)
    for comp in range(3):
        diff = target[comp][..., :, None] - source[comp][..., None, :]
        square = square + diff * diff
    return 1.0 / jnp.sqrt(square + softening)

def near_term(target, source, values, weight):
    tile = kernel_block(target, source) * weight.astype(jnp.float32)[:, :, None, None]
    return jnp.einsum('abij,sabj->sabi', tile, values, precision=lax.Precision.HIGHEST)

def inverse_order(order):
    flat = order.reshape(-1, order.shape[-1])
    iota = jnp.broadcast_to(jnp.arange(flat.shape[1], dtype=jnp.int32)[None, :], flat.shape)
    lines = jnp.broadcast_to(jnp.arange(flat.shape[0], dtype=jnp.int32)[:, None], flat.shape)
    inverse = jnp.zeros_like(flat).at[lines, flat].set(iota)
    return inverse.reshape(order.shape)

def reference(vectors, leaf_order, offsets, near_mask, far_mask, basis, transfer, coupling, top_coupling, cluster_owner):
    hp = lax.Precision.HIGHEST
    sorted_vec = jnp.take_along_axis(vectors, leaf_order[None], axis=3)
    row_pos = jnp.arange(LEAFR, dtype=jnp.float32)[:, None, None] + offsets[0]
    col_pos = jnp.arange(LEAFC, dtype=jnp.float32)[None, :, None] + offsets[1]
    pos = jnp.stack([row_pos, col_pos, 0.25 * offsets[2]], 0)
    pad_spec = ((0, 0), (1, 1), (1, 1), (0, 0))
    pos_pad = jnp.pad(pos, pad_spec)
    vec_pad = jnp.pad(sorted_vec, pad_spec)

    def near_row(line):
        target = lax.dynamic_slice_in_dim(pos, line, 1, 1)
        total = jnp.zeros((RHS, 1, LEAFC, LEAF), jnp.float32)
        for down_step in (-1, 0, 1):
            for right_step in (-1, 0, 1):
                slot = 3 * (down_step + 1) + right_step + 1
                source = lax.dynamic_slice_in_dim(pos_pad, line + 1 + down_step, 1, 1)[:, :, 1 + right_step:1 + right_step + LEAFC]
                values = lax.dynamic_slice_in_dim(vec_pad, line + 1 + down_step, 1, 1)[:, :, 1 + right_step:1 + right_step + LEAFC]
                weight = lax.dynamic_slice_in_dim(near_mask[slot], line, 1, 0)
                total = total + near_term(target, source, values, weight)
        return total[:, 0]
    lines_out = lax.map(near_row, jnp.arange(LEAFR, dtype=jnp.int32))
    near = jnp.transpose(lines_out, (1, 0, 2, 3)) * (1.0 / (3.0 * math.sqrt(LEAF)))
    coef = jnp.einsum('abkp,sabp->ksab', basis, sorted_vec, precision=hp)
    coef_pad = jnp.pad(coef, ((0, 0), (0, 0), (2, 2), (2, 2)))
    far = jnp.zeros_like(coef)
    for slot, (down_step, right_step) in enumerate(far_offsets()):
        window = coef_pad[:, :, 2 + down_step:2 + down_step + LEAFR, 2 + right_step:2 + right_step + LEAFC]
        moved = jnp.einsum('jk,ksab->jsab', coupling[slot], window, precision=hp)
        far = far + moved * far_mask[slot].astype(jnp.float32)[None, None]
    shaped_transfer = transfer.reshape(N_ROW, LR, N_COL, LC, RANK, RANK)
    shaped_coef = coef.reshape(RANK, RHS, N_ROW, LR, N_COL, LC)
    cluster = jnp.einsum('xaybkj,ksxayb->xyjs', shaped_transfer, shaped_coef, precision=hp)
    nodes = jnp.arange(TOPN, dtype=jnp.int32)
    onehot = (cluster_owner[None] == nodes[:, None, None]).astype(jnp.float32)
    top = jnp.einsum('gxy,xyjs->gjs', onehot, cluster, precision=hp)
    table = top_coupling[(nodes[:, None] - nodes[None, :]) % TOPN]
    keep = (nodes[:, None] != nodes[None, :]).astype(jnp.float32)
    top_local = jnp.einsum('gh,ghjk,hks->gjs', keep, table, top, precision=hp)
    device_local = jnp.einsum('gxy,gjs->xyjs', onehot, top_local, precision=hp)
    down = jnp.einsum('xaybkj,xyjs->ksxayb', shaped_transfer, device_local, precision=hp)
    local = far + down.reshape(RANK, RHS, LEAFR, LEAFC)
    result = near + jnp.einsum('abkp,ksab->sabp', basis, local, precision=hp)
    return jnp.take_along_axis(result, inverse_order(leaf_order)[None], axis=3)
```

```python
import functools

import jax
import jax.numpy as jnp
from jax import lax
from jax.experimental import pallas as pl
from jax.experimental.pallas import tpu as pltpu
from jax.sharding import PartitionSpec as P

F32, BF16 = jnp.float32, jnp.bfloat16
MESH = pl.DeviceIdType.MESH
RHS, LR, LC, LEAF, RANK, TOPN = 16, 2, 8, 256, 64, 16
WIDE = LC + 2
REC = 40
softening = 0.01

NN = (((1,), (0,)), ((), ()))
NT = (((1,), (1,)), ((), ()))
TN = (((0,), (0,)), ((), ()))


def far_offsets():
    return [(i, j) for i in range(-2, 3) for j in range(-2, 3) if max(abs(i), abs(j)) == 2]


def dot(a, b, dims=NN):
    return lax.dot_general(a, b, dims, preferred_element_type=F32)


def split2(x):
    hi = x.astype(BF16)
    return hi, (x - hi.astype(F32)).astype(BF16)


def split3(x):
    a = x.astype(BF16).astype(F32)
    r = x - a
    b = r.astype(BF16).astype(F32)
    return a, b, r - b


def kernel(
    dims,
    vec,
    order,
    off,
    nmask,
    fmask,
    basis,
    transfer,
    coupling,
    topc,
    owner_ref,
    out,
    vin,
    vout,
    io_sem,
    nw,
    cw,
    perm,
    bh,
    bl,
    th,
    tl,
    lead,
    feat,
    qt,
    vhl,
    wf,
    wt,
    gp,
    nacc,
    eh,
    el,
    am,
    send_a,
    recv_a,
    mine_y,
    recv_y,
    mine_z,
    recv_z,
    recv_c,
    nsend,
    nrecv,
    csend,
    crecv,
    asend,
    arecv,
    ysend,
    yrecv,
    zsend,
    zrecv,
    dsend,
    drecv,
):
    nx, nzl, ny, nzh, nc = dims
    rows_n, cols_n = nzh * nc, nx * nzl * ny
    group, nz = nx * nc, nzh * nzl
    row, col = lax.axis_index("row"), lax.axis_index("col")
    zh, core = row // nc, row % nc
    x, zl, y = col // (nzl * ny), (col // ny) % nzl, col % ny
    me_g, me_z = x * nc + core, zh * nzl + zl

    def member(i):
        return (zh * nc + i % nc, (i // nc) * (nzl * ny) + zl * ny + y)

    def along_y(i):
        return (row, x * (nzl * ny) + zl * ny + i)

    def along_z(i):
        return ((i // nzl) * nc + core, x * (nzl * ny) + (i % nzl) * ny + y)

    def beside(dr, dc):
        return ((row + dr + rows_n) % rows_n, (col + dc + cols_n) % cols_n)

    half = [slice(0, 128), slice(128, 256)]
    loads = [pltpu.make_async_copy(vec.at[:, half[h]], vin.at[h], io_sem.at[h]) for h in range(2)]
    for copy in loads:
        copy.start()

    around = [(i, j) for i in (-1, 0, 1) for j in (-1, 0, 1) if (i, j) != (0, 0)]
    barrier = pltpu.get_barrier_semaphore()

    def greet(device):
        pl.semaphore_signal(barrier, inc=1, device_id=device, device_id_type=MESH)

    @pl.loop(1, group)
    def _(i):
        greet(member((me_g + i) % group))

    @pl.loop(1, ny)
    def _(i):
        greet(along_y((y + i) % ny))

    @pl.loop(1, nz)
    def _(i):
        greet(along_z((me_z + i) % nz))

    for step in around:
        greet(beside(*step))

    low_lanes = lax.broadcasted_iota(jnp.int32, (8, 128), 1) < RANK
    low_lanes16 = lax.broadcasted_iota(jnp.int32, (16, 128), 1) < RANK
    owner = owner_ref[0, 0]

    def spread(tile):
        return jnp.concatenate(
            [jnp.where(low_lanes, tile, 0.0), jnp.where(low_lanes, 0.0, tile)], 0
        )

    base = lax.broadcasted_iota(jnp.int32, (LR * LC, LEAF), 0)
    row_first = (row * LR + base // LC).astype(F32)
    col_first = (col * LC + base % LC).astype(F32)
    px = ((row_first + off[0:16, :]) - row_first) - 0.5
    py = ((col_first + off[16:32, :]) - col_first) - 0.5
    pz = 0.25 * off[32:48, :] - 0.125
    pn = (px * px + py * py + pz * pz) + softening
    for r in range(LR):
        first = ((1 + r) * WIDE + 1) * REC + 32
        for h in range(2):
            for c, value in enumerate((px, py, pz, pn)):
                nw[pl.ds(first + 4 * h + c, LC, stride=REC), :] = value[
                    r * LC : (r + 1) * LC, h * 128 : (h + 1) * 128
                ]

    def rec_of(wide):
        return pl.multiple_of(wide * REC, 8)

    @pl.loop(0, LR * LC)
    def _(t):
        k = pl.ds(pl.multiple_of(t * RANK, RANK), RANK)
        bh[k, :], bl[k, :] = split2(basis[k, :])
        th[k, :], tl[k, :] = split2(transfer[k, :])

    for copy in loads:
        copy.wait()
    lane_q = lax.broadcasted_iota(jnp.int32, (LEAF, LEAF), 0)

    def sort_leaf(t):
        hot = jnp.where(lane_q == order[pl.ds(t, 1), :], 1.0, 0.0).astype(BF16)
        perm[t] = hot
        v = jnp.concatenate(
            [vin[h, pl.ds(t, 16, stride=16), :] for h in range(2)], 1
        )
        parts = dot(jnp.concatenate(split2(v), 0), hot)
        wide = (1 + t // LC) * WIDE + 1 + t % LC
        at = rec_of(wide)
        for h in range(2):
            both = parts[:16, h * 128 : (h + 1) * 128] + parts[16:, h * 128 : (h + 1) * 128]
            nw[pl.ds(at + 16 * h, 16), :] = both
        sorted2 = parts.astype(BF16)
        vhl[wide] = sorted2
        k = pl.ds(pl.multiple_of(t * RANK, RANK), RANK)
        both = jnp.concatenate([bh[k, :], bl[k, :]], 0)
        c4 = dot(sorted2, both, NT)
        c2 = c4[:16] + c4[16:]
        c = c2 + pltpu.roll(c2, RANK, 1)
        cw[2 + t // LC, 2 + t % LC] = jnp.where(low_lanes, c[:8], c[8:])
        return c

    @pl.loop(0, LR * LC // 2)
    def _(i):
        c = jnp.where(low_lanes16, sort_leaf(2 * i), sort_leaf(2 * i + 1))
        hi, lo = split2(c)
        lead[:, pl.ds(pl.multiple_of(i * 128, 128), 128)] = jnp.concatenate([hi, lo], 0)

    cl = dot(lead[...], th[...])
    cl = (cl[:16] + cl[16:]) + dot(lead[0:16, :], tl[...])
    packed = jnp.concatenate([cl[:8], cl[8:]], 1)
    slots = TOPN // group
    for g in range(group):
        for s in range(slots):
            send_a[g, 8 * s : 8 * s + 8, :] = jnp.where(owner == g * slots + s, packed, 0.0)

    def near_copies():
        found = []
        for n, (dr, dc) in enumerate(around):
            rs = {-1: [1], 0: [1, 2], 1: [2]}[dr]
            c0, count = {-1: (1, 1), 0: (1, LC), 1: (LC, 1)}[dc]
            for r in rs:
                r_to = r - 2 * dr
                c_to = c0 - LC * dc
                found.append((
                    nw.at[pl.ds((r * WIDE + c0) * REC, count * REC)],
                    nw.at[pl.ds((r_to * WIDE + c_to) * REC, count * REC)],
                    (dr, dc),
                ))
        return [
            pltpu.make_async_remote_copy(
                a, b, nsend.at[n], nrecv.at[n], device_id=beside(*s), device_id_type=MESH
            )
            for n, (a, b, s) in enumerate(found)
        ]

    def coef_copies():
        found = []
        for dr, dc in around:
            c0, count = {-1: (2, 2), 0: (2, LC), 1: (LC, 2)}[dc]
            r_to, c_to = 2 - 2 * dr, c0 - LC * dc
            found.append((
                cw.at[2:4, c0 : c0 + count],
                cw.at[r_to : r_to + 2, c_to : c_to + count],
                (dr, dc),
            ))
        return [
            pltpu.make_async_remote_copy(
                a, b, csend.at[n], crecv.at[n], device_id=beside(*s), device_id_type=MESH
            )
            for n, (a, b, s) in enumerate(found)
        ]

    def copy_a(i):
        to = (me_g + i) % group
        return pltpu.make_async_remote_copy(
            send_a.at[to], recv_a.at[i], asend.at[i], arecv.at[i],
            device_id=member(to), device_id_type=MESH,
        )

    def copy_y(i):
        return pltpu.make_async_remote_copy(
            mine_y, recv_y.at[i], ysend.at[i], yrecv.at[i],
            device_id=along_y((y + i) % ny), device_id_type=MESH,
        )

    def copy_z(i):
        return pltpu.make_async_remote_copy(
            mine_z, recv_z.at[i], zsend.at[i], zrecv.at[i],
            device_id=along_z((me_z + i) % nz), device_id_type=MESH,
        )

    def copy_c(i):
        return pltpu.make_async_remote_copy(
            recv_c.at[0], recv_c.at[i], dsend.at[i], drecv.at[i],
            device_id=member((me_g + i) % group), device_id_type=MESH,
        )

    def every(count, copy, act):
        @pl.loop(1, count)
        def _(i):
            act(copy(i))

    start, arrived, left = (lambda c: c.start()), (lambda c: c.wait_recv()), (lambda c: c.wait_send())

    pl.semaphore_wait(barrier, (group - 1) + (ny - 1) + (nz - 1) + len(around))
    every(group, copy_a, start)
    for copy in near_copies():
        copy.start()
    for copy in coef_copies():
        copy.start()

    lane_row = lax.broadcasted_iota(jnp.int32, (8, LEAF), 0)

    def features(wide, own):
        at = rec_of(wide)
        tile = nw[pl.ds(at + 32, 8), :]
        f = jnp.concatenate([tile, pltpu.roll(tile, 4, 0)], 1)
        f = jnp.where(lane_row < 4, f, jnp.where(lane_row == 4, 1.0, 0.0))
        if own is not None:
            feat[own] = f
        a, b, c = split3(f)
        q = jnp.concatenate([a, a, a, b, b, c], 0)
        qt[wide] = jnp.transpose(q).astype(BF16)
        if own is None:
            v = jnp.concatenate([nw[pl.ds(at, 16), :], nw[pl.ds(at + 16, 16), :]], 1)
            vhl[wide] = jnp.concatenate(split2(v), 0)

    @pl.loop(0, LR * LC)
    def _(t):
        features((1 + t // LC) * WIDE + 1 + t % LC, t)

    def near_pair(f, a, b, da, db):
        d = f - jnp.where(lane_row == 0, float(da), jnp.where(lane_row == 1, float(db), 0.0))
        sq = d * d
        m = sq[0:1] + sq[1:2] + sq[2:3]
        d = jnp.where(
            lane_row < 3,
            -2.0 * d,
            jnp.where(lane_row == 3, 1.0, jnp.where(lane_row == 4, m, 0.0)),
        )
        d1, d2, d3 = split3(d)
        p = jnp.concatenate([d1, d2, d3, d1, d2, d1], 0).astype(BF16)
        wide = (1 + a + da) * WIDE + 1 + b + db
        g = lax.rsqrt(dot(qt[wide], p))
        gh, gl = split2(g)
        v = vhl[wide]
        o = dot(v, gh)
        o = (o[:16] + o[16:]) + dot(v[:16], gl)
        r, c = row * LR + a + da, col * LC + b + db
        inside = (r >= 0) & (r < rows_n * LR) & (c >= 0) & (c < cols_n * LC)
        on = nmask[3 * (da + 1) + db + 1, a, b].astype(F32) * jnp.where(inside, 1.0, 0.0)
        return o * on

    def near_group(a, b, das):
        f = feat[a * LC + b]
        total = None
        for da in das:
            for db in (-1, 0, 1):
                term = near_pair(f, a, b, da, db)
                total = term if total is None else total + term
        return total

    def near_own(b):
        nacc[b] = near_group(0, b, (0, 1))
        nacc[LC + b] = near_group(1, b, (-1, 0))

    def near_outer(b):
        nacc[b] += near_group(0, b, (-1,))
        nacc[LC + b] += near_group(1, b, (1,))

    for o in range(0, 16):
        k = slice(o * RANK, (o + 1) * RANK)
        hi, lo = split2(coupling[k, :])
        w = jnp.concatenate([hi, lo], 0)
        wf[o // 2, :, (o % 2) * 128 : (o % 2) * 128 + 128] = jnp.concatenate([w, w], 1)
    for d in range(16):
        k = slice(d * RANK, (d + 1) * RANK)
        hi, lo = split2(topc[k, :])
        w = jnp.concatenate([hi, lo], 0)
        wt[d // 2, :, (d % 2) * 128 : (d % 2) * 128 + 128] = jnp.concatenate([w, w], 1)

    @pl.loop(1, 3)
    def _(b):
        near_own(b)

    every(group, copy_a, arrived)
    total = send_a[me_g]
    for i in range(1, group):
        total = total + recv_a[i]
    mine_y[...] = total
    every(ny, copy_y, start)

    @pl.loop(3, 5)
    def _(b):
        near_own(b)

    @pl.loop(0, LR * LC)
    def _(t):
        k = pl.ds(pl.multiple_of(t * RANK, RANK), RANK)
        tt = jnp.transpose(transfer[k, :])
        thi, tlo = split2(tt)
        q = dot(jnp.concatenate([thi, tlo], 0), bh[k, :])
        q = (q[:RANK] + q[RANK:]) + dot(thi, bl[k, :])
        hi, lo = split2(q)
        gp[t] = dot(jnp.concatenate([hi, lo], 0), perm[t], NT).astype(BF16)

    every(ny, copy_y, arrived)
    total = mine_y[...]
    for i in range(1, ny):
        total = total + recv_y[i]
    mine_z[...] = total
    every(nz, copy_z, start)

    @pl.loop(5, 7)
    def _(b):
        near_own(b)

    for copy in near_copies():
        copy.wait_recv()
    for copy in coef_copies():
        copy.wait_recv()
    for r in (0, 3):

        @pl.loop(0, WIDE)
        def _(c):
            features(r * WIDE + c, None)

    for r in (1, 2):
        for c in (0, WIDE - 1):
            features(r * WIDE + c, None)

    @pl.loop(0, 2)
    def _(i):
        near_own(i * (LC - 1))

    every(nz, copy_z, arrived)
    total = mine_z[...]
    for i in range(1, nz):
        total = total + recv_z[i]
    recv_c[0] = total
    every(group, copy_c, start)

    for r in range(LR + 4):

        @pl.loop(0, LC + 4)
        def _(c):
            hi, lo = split2(spread(cw[r, c]))
            eh[r, c] = hi
            el[r, c] = lo

    for o, (da, db) in enumerate(far_offsets()):

        @pl.loop(0, LC)
        def _(b):
            for a in range(LR):
                r, c = row * LR + a + da, col * LC + b + db
                inside = (r >= 0) & (r < rows_n * LR) & (c >= 0) & (c < cols_n * LC)
                on = fmask[o, a, b].astype(F32) * jnp.where(inside, 1.0, 0.0)
                on = jnp.full((16, 128), on, F32).astype(BF16)
                lanes = slice((o % 2) * 128, (o % 2) * 128 + 128)
                at = pl.multiple_of((a * LC + b) * 16, 16)
                am[o // 2, pl.ds(at, 16), lanes] = eh[2 + a + da, 2 + b + db] * on
                am[o // 2, pl.ds(at + 256, 16), lanes] = el[2 + a + da, 2 + b + db] * on

    far = dot(am[0], wf[0], NT)
    for o in range(1, 8):
        far = far + dot(am[o], wf[o], NT)
    far = far[:256] + far[256:]
    far = far + pltpu.roll(far, RANK, 1)
    fh, fl = split2(far)
    eh_far, el_far = fh, fl
    am[0, 0:256, 0:128] = eh_far
    am[0, 256:512, 0:128] = el_far

    @pl.loop(0, LC)
    def _(b):
        near_outer(b)

    @pl.loop(0, LR * LC)
    def _(t):
        k = pl.ds(pl.multiple_of(t * RANK, RANK), RANK)
        at = pl.multiple_of(t * 16, 16)
        f_hi, f_lo = am[0, pl.ds(at, 16), 0:RANK], am[0, pl.ds(at + 256, 16), 0:RANK]
        q = dot(jnp.concatenate([f_hi, f_lo], 0), bh[k, :])
        q = (q[:16] + q[16:]) + dot(f_hi, bl[k, :])
        q = q + nacc[t] * (1.0 / 48.0)
        q = dot(jnp.concatenate(split2(q), 0), perm[t], NT)
        nacc[t] = q[:16] + q[16:]

    every(group, copy_c, arrived)
    acc = None
    for pair in range(8):
        parts = []
        for d in (2 * pair, 2 * pair + 1):
            h = (owner - d + TOPN) % TOPN
            m = (me_g - h // slots + group) % group
            tile = recv_c[m, pl.ds(0, 8), :] if slots == 1 else recv_c[m, pl.ds(pl.multiple_of((h % slots) * 8, 8), 8), :]
            if d == 0:
                tile = jnp.zeros_like(tile)
            parts.append(spread(tile))
        hi, lo = split2(jnp.concatenate(parts, 1))
        term = dot(jnp.concatenate([hi, lo], 0), wt[pair], NT)
        acc = term if acc is None else acc + term
    acc = acc[:16] + acc[16:]
    acc = acc + pltpu.roll(acc, RANK, 1)
    hi, lo = split2(acc)
    zero = jnp.zeros_like(acc)
    dl = jnp.concatenate(
        [hi.astype(F32), jnp.where(low_lanes16, lo.astype(F32), zero)], 0
    ).astype(BF16)

    @pl.loop(0, LR * LC)
    def _(t):
        q = dot(dl, gp[t])
        q = (q[:16] + q[16:]) + nacc[t]
        for h in range(2):
            vout[h, pl.ds(t, 16, stride=16), :] = q[:, h * 128 : (h + 1) * 128]

    stores = [pltpu.make_async_copy(vout.at[h], out.at[:, half[h]], io_sem.at[h]) for h in range(2)]
    for copy in stores:
        copy.start()

    every(group, copy_a, left)
    every(ny, copy_y, left)
    every(nz, copy_z, left)
    every(group, copy_c, left)
    for copy in near_copies():
        copy.wait_send()
    for copy in coef_copies():
        copy.wait_send()
    for copy in stores:
        copy.wait()


def on_device(
    dims,
    vectors,
    leaf_order,
    offsets,
    near_mask,
    far_mask,
    basis,
    transfer,
    coupling,
    top_coupling,
    cluster_owner,
):
    nx, nzl, ny, nzh, nc = dims
    group, nz = nx * nc, nzh * nzl
    slots = TOPN // group
    vmem = pl.BlockSpec(memory_space=pltpu.VMEM)
    smem = pl.BlockSpec(memory_space=pltpu.SMEM)
    dma = pltpu.SemaphoreType.DMA
    result = pl.pallas_call(
        functools.partial(kernel, dims),
        out_shape=jax.ShapeDtypeStruct((RHS * LR * LC, LEAF), F32),
        in_specs=[pl.BlockSpec(memory_space=pl.ANY), vmem, vmem, smem, smem, vmem, vmem, vmem, vmem, smem],
        out_specs=pl.BlockSpec(memory_space=pl.ANY),
        scratch_shapes=[
            pltpu.VMEM((2, 256, 128), F32),
            pltpu.VMEM((2, 256, 128), F32),
            dma((2,)),
            pltpu.VMEM((4 * WIDE * REC, 128), F32),
            pltpu.VMEM((LR + 4, LC + 4, 8, 128), F32),
            pltpu.VMEM((16, LEAF, LEAF), BF16),
            pltpu.VMEM((1024, LEAF), BF16),
            pltpu.VMEM((1024, LEAF), BF16),
            pltpu.VMEM((1024, RANK), BF16),
            pltpu.VMEM((1024, RANK), BF16),
            pltpu.VMEM((32, 1024), BF16),
            pltpu.VMEM((16, 8, LEAF), F32),
            pltpu.VMEM((4 * WIDE, LEAF, 48), BF16),
            pltpu.VMEM((4 * WIDE, 32, LEAF), BF16),
            pltpu.VMEM((8, 128, 256), BF16),
            pltpu.VMEM((8, 128, 256), BF16),
            pltpu.VMEM((16, 128, LEAF), BF16),
            pltpu.VMEM((16, 16, LEAF), F32),
            pltpu.VMEM((LR + 4, LC + 4, 16, 128), BF16),
            pltpu.VMEM((LR + 4, LC + 4, 16, 128), BF16),
            pltpu.VMEM((8, 512, 256), BF16),
            pltpu.VMEM((group, 8 * slots, 128), F32),
            pltpu.VMEM((group, 8 * slots, 128), F32),
            pltpu.VMEM((8 * slots, 128), F32),
            pltpu.VMEM((ny, 8 * slots, 128), F32),
            pltpu.VMEM((8 * slots, 128), F32),
            pltpu.VMEM((nz, 8 * slots, 128), F32),
            pltpu.VMEM((group, 8 * slots, 128), F32),
            dma((10,)),
            dma((10,)),
            dma((8,)),
            dma((8,)),
            dma((group,)),
            dma((group,)),
            dma((ny,)),
            dma((ny,)),
            dma((nz,)),
            dma((nz,)),
            dma((group,)),
            dma((group,)),
        ],
        compiler_params=pltpu.CompilerParams(
            collective_id=0, has_side_effects=True, vmem_limit_bytes=48 << 20
        ),
        name="operator",
    )(
        vectors.reshape(RHS * LR * LC, LEAF),
        leaf_order.reshape(LR * LC, LEAF),
        offsets.reshape(3 * LR * LC, LEAF),
        near_mask,
        far_mask,
        basis.reshape(LR * LC * RANK, LEAF),
        transfer.reshape(LR * LC * RANK, RANK),
        coupling.reshape(16 * RANK, RANK),
        top_coupling.reshape(TOPN * RANK, RANK),
        cluster_owner,
    )
    return result.reshape(RHS, LR, LC, LEAF)


def solution(mesh, dims=(8, 2, 8, 4, 2)):
    in_specs = (
        P(None, "row", "col", None),
        P("row", "col", None),
        P(None, "row", "col", None),
        P(None, "row", "col"),
        P(None, "row", "col"),
        P("row", "col", None, None),
        P("row", "col", None, None),
        P(),
        P(),
        P("row", "col"),
    )
    out_specs = P(None, "row", "col", None)
    return jax.shard_map(
        functools.partial(on_device, dims),
        mesh=mesh,
        in_specs=in_specs,
        out_specs=out_specs,
        check_vma=False,
    )
```

```python
import functools

import jax
import jax.numpy as jnp
from jax import lax
from jax.experimental import pallas as pl
from jax.experimental.pallas import tpu as pltpu
from jax.sharding import PartitionSpec as P

F32, BF16 = jnp.float32, jnp.bfloat16
MESH = pl.DeviceIdType.MESH
RHS, LR, LC, LEAF, RANK, TOPN = 16, 2, 8, 256, 64, 16
WIDE = LC + 2
REC = 40
softening = 0.01

CHUNKS = 4
UNROLL = LR * LC // CHUNKS
AHEAD = 3
PLAN = dict(enter=("wfng", ""), a=("m", "wfm"), y=("h", "h"), z=("la", "la"), c=("ebr", "ngebr"))

NN = (((1,), (0,)), ((), ()))
NT = (((1,), (1,)), ((), ()))
TN = (((0,), (0,)), ((), ()))


def far_offsets():
    return [(i, j) for i in range(-2, 3) for j in range(-2, 3) if max(abs(i), abs(j)) == 2]


def dot(a, b, dims=NN):
    return lax.dot_general(a, b, dims, preferred_element_type=F32)


def split2(x):
    hi = x.astype(BF16)
    return hi, (x - hi.astype(F32)).astype(BF16)


def split3(x):
    a = x.astype(BF16).astype(F32)
    r = x - a
    b = r.astype(BF16).astype(F32)
    return a, b, r - b


def kernel(
    dims,
    vec,
    order_in,
    off_in,
    nmask_in,
    fmask_in,
    basis_in,
    transfer_in,
    coupling_in,
    topc_in,
    owner_in,
    out,
    vin,
    vout,
    order,
    off,
    basis,
    transfer,
    coupling,
    topc,
    nmask,
    fmask,
    owner_ref,
    io_sem,
    nw,
    cw,
    perm,
    bh,
    bl,
    th,
    tl,
    lead,
    feat,
    qt,
    vhl,
    wf,
    wt,
    gp,
    nacc,
    eh,
    el,
    am,
    send_a,
    recv_a,
    mine_y,
    recv_y,
    mine_z,
    recv_z,
    recv_c,
    nsend,
    nrecv,
    csend,
    crecv,
    asend,
    arecv,
    ysend,
    yrecv,
    zsend,
    zrecv,
    dsend,
    drecv,
):
    nx, nzl, ny, nzh, nc = dims
    rows_n, cols_n = nzh * nc, nx * nzl * ny
    group, nz = nx * nc, nzh * nzl
    row, col = lax.axis_index("row"), lax.axis_index("col")
    zh, core = row // nc, row % nc
    x, zl, y = col // (nzl * ny), (col // ny) % nzl, col % ny
    me_g, me_z = x * nc + core, zh * nzl + zl

    def member(i):
        return (zh * nc + i % nc, (i // nc) * (nzl * ny) + zl * ny + y)

    def along_y(i):
        return (row, x * (nzl * ny) + zl * ny + i)

    def along_z(i):
        return ((i // nzl) * nc + core, x * (nzl * ny) + (i % nzl) * ny + y)

    def beside(dr, dc):
        return ((row + dr + rows_n) % rows_n, (col + dc + cols_n) % cols_n)

    half = [slice(0, 128), slice(128, 256)]
    moves = [
        (order_in, order),
        (vec.at[:, half[0]], vin.at[0]),
        (vec.at[:, half[1]], vin.at[1]),
    ]
    part = LR * LC * RANK // CHUNKS
    moves += [(basis_in.at[pl.ds(n * part, part)], basis.at[pl.ds(n * part, part)]) for n in range(CHUNKS)]
    late = len(moves)
    moves += [
        (off_in, off),
        (transfer_in, transfer),
        (owner_in, owner_ref),
        (nmask_in, nmask),
        (fmask_in, fmask),
        (topc_in, topc),
        (coupling_in, coupling),
    ]
    loads = [pltpu.make_async_copy(a, b, io_sem.at[n]) for n, (a, b) in enumerate(moves)]
    for copy in loads:
        copy.start()

    around = [(i, j) for i in (-1, 0, 1) for j in (-1, 0, 1) if (i, j) != (0, 0)]
    barrier = pltpu.get_barrier_semaphore()

    def greet(device):
        pl.semaphore_signal(barrier, inc=1, device_id=device, device_id_type=MESH)

    @pl.loop(1, group)
    def _(i):
        greet(member((me_g + i) % group))

    @pl.loop(1, ny)
    def _(i):
        greet(along_y((y + i) % ny))

    @pl.loop(1, nz)
    def _(i):
        greet(along_z((me_z + i) % nz))

    for step in around:
        greet(beside(*step))

    nacc[...] = jnp.zeros_like(nacc)
    low_lanes = lax.broadcasted_iota(jnp.int32, (8, 128), 1) < RANK
    low_lanes16 = lax.broadcasted_iota(jnp.int32, (16, 128), 1) < RANK

    def spread(tile):
        return jnp.concatenate(
            [jnp.where(low_lanes, tile, 0.0), jnp.where(low_lanes, 0.0, tile)], 0
        )

    def rec_of(wide):
        return pl.multiple_of(wide * REC, 8)

    for n in range(3):
        loads[n].wait()
    lane_q = lax.broadcasted_iota(jnp.int32, (LEAF, LEAF), 0)

    def sort_leaf(t):
        hot = jnp.where(lane_q == order[pl.ds(t, 1), :], 1.0, 0.0).astype(BF16)
        perm[t] = hot
        v = jnp.concatenate(
            [vin[h, pl.ds(t, 16, stride=16), :] for h in range(2)], 1
        )
        parts = dot(jnp.concatenate(split2(v), 0), hot)
        wide = (1 + t // LC) * WIDE + 1 + t % LC
        at = rec_of(wide)
        for h in range(2):
            both = parts[:16, h * 128 : (h + 1) * 128] + parts[16:, h * 128 : (h + 1) * 128]
            nw[pl.ds(at + 16 * h, 16), :] = both
        sorted2 = parts.astype(BF16)
        vhl[wide] = sorted2
        k = pl.ds(pl.multiple_of(t * RANK, RANK), RANK)
        hi, lo = split2(basis[k, :])
        bh[k, :], bl[k, :] = hi, lo
        c4 = dot(sorted2, jnp.concatenate([hi, lo], 0), NT)
        c2 = c4[:16] + c4[16:]
        c = c2 + pltpu.roll(c2, RANK, 1)
        cw[2 + t // LC, 2 + t % LC] = jnp.where(low_lanes, c[:8], c[8:])
        return c

    @pl.loop(0, CHUNKS)
    def _(i):
        rows = pl.ds(pl.multiple_of(i * part, part), part)
        pltpu.make_async_copy(basis_in.at[rows], basis.at[rows], io_sem.at[3 + i]).wait()
        cs = [sort_leaf(UNROLL * i + n) for n in range(UNROLL)]
        for n in range(0, UNROLL, 2):
            hi, lo = split2(jnp.where(low_lanes16, cs[n], cs[n + 1]))
            at = pl.multiple_of(i * (UNROLL * RANK) + n * RANK, 128)
            lead[:, pl.ds(at, 128)] = jnp.concatenate([hi, lo], 0)

    loads[late + 1].wait()
    loads[late + 2].wait()
    owner = owner_ref[0, 0]
    th[...], tl[...] = split2(transfer[...])
    cl = dot(lead[...], th[...])
    cl = (cl[:16] + cl[16:]) + dot(lead[0:16, :], tl[...])
    packed = jnp.concatenate([cl[:8], cl[8:]], 1)
    slots = TOPN // group
    for g in range(group):
        for s in range(slots):
            send_a[g, 8 * s : 8 * s + 8, :] = jnp.where(owner == g * slots + s, packed, 0.0)

    loads[late].wait()
    base = lax.broadcasted_iota(jnp.int32, (LR * LC, LEAF), 0)
    row_first = (row * LR + base // LC).astype(F32)
    col_first = (col * LC + base % LC).astype(F32)
    px = ((row_first + off[0:16, :]) - row_first) - 0.5
    py = ((col_first + off[16:32, :]) - col_first) - 0.5
    pz = 0.25 * off[32:48, :] - 0.125
    pn = (px * px + py * py + pz * pz) + softening
    for r in range(LR):
        first = ((1 + r) * WIDE + 1) * REC + 32
        for h in range(2):
            for c, value in enumerate((px, py, pz, pn)):
                nw[pl.ds(first + 4 * h + c, LC, stride=REC), :] = value[
                    r * LC : (r + 1) * LC, h * 128 : (h + 1) * 128
                ]

    def near_copies():
        found = []
        for n, (dr, dc) in enumerate(around):
            rs = {-1: [1], 0: [1, 2], 1: [2]}[dr]
            c0, count = {-1: (1, 1), 0: (1, LC), 1: (LC, 1)}[dc]
            for r in rs:
                r_to = r - 2 * dr
                c_to = c0 - LC * dc
                found.append((
                    nw.at[pl.ds((r * WIDE + c0) * REC, count * REC)],
                    nw.at[pl.ds((r_to * WIDE + c_to) * REC, count * REC)],
                    (dr, dc),
                ))
        return [
            pltpu.make_async_remote_copy(
                a, b, nsend, nrecv, device_id=beside(*s), device_id_type=MESH
            )
            for n, (a, b, s) in enumerate(found)
        ]

    def coef_copies():
        found = []
        for dr, dc in around:
            c0, count = {-1: (2, 2), 0: (2, LC), 1: (LC, 2)}[dc]
            r_to, c_to = 2 - 2 * dr, c0 - LC * dc
            found.append((
                cw.at[2:4, c0 : c0 + count],
                cw.at[r_to : r_to + 2, c_to : c_to + count],
                (dr, dc),
            ))
        return [
            pltpu.make_async_remote_copy(
                a, b, csend, crecv, device_id=beside(*s), device_id_type=MESH
            )
            for n, (a, b, s) in enumerate(found)
        ]

    def copy_a(i):
        to = (me_g + i) % group
        return pltpu.make_async_remote_copy(
            send_a.at[to], recv_a.at[i], asend, arecv,
            device_id=member(to), device_id_type=MESH,
        )

    def copy_y(i):
        return pltpu.make_async_remote_copy(
            mine_y, recv_y.at[i], ysend, yrecv,
            device_id=along_y((y + i) % ny), device_id_type=MESH,
        )

    def copy_z(i):
        return pltpu.make_async_remote_copy(
            mine_z, recv_z.at[i], zsend, zrecv,
            device_id=along_z((me_z + i) % nz), device_id_type=MESH,
        )

    def copy_c(i):
        return pltpu.make_async_remote_copy(
            recv_c.at[0], recv_c.at[i], dsend, drecv,
            device_id=member((me_g + i) % group), device_id_type=MESH,
        )

    def sent(copy, count):
        for i in sorted(range(1, count), key=lambda i: abs(2 * i - count)):
            copy(i).start()

    def done(sem, ref):
        pltpu.make_async_copy(ref, ref, sem).wait()

    near_bytes = nw.at[pl.ds(0, (4 * WIDE - LR * LC) * REC)]
    coef_bytes = nw.at[pl.ds(0, ((LR + 4) * (LC + 4) - LR * LC) * 8)]
    member_bytes = recv_a.at[pl.ds(1, group - 1)]
    y_bytes = recv_y.at[pl.ds(1, ny - 1)]
    z_bytes = recv_z.at[pl.ds(1, nz - 1)]

    lane_row = lax.broadcasted_iota(jnp.int32, (8, LEAF), 0)

    def inside(r, c):
        r, c = row * LR + r, col * LC + c
        ok = (r >= 0) & (r < rows_n * LR) & (c >= 0) & (c < cols_n * LC)
        return jnp.where(ok, 1.0, 0.0)

    def features(wide, own):
        at = rec_of(wide)
        tile = nw[pl.ds(at + 32, 8), :]
        f = jnp.concatenate([tile, pltpu.roll(tile, 4, 0)], 1)
        f = jnp.where(lane_row < 4, f, jnp.where(lane_row == 4, 1.0, 0.0))
        if own is not None:
            feat[own] = f
        a, b, c = split3(f)
        q = jnp.concatenate([a, a, a, b, b, c], 0)
        qt[wide] = jnp.transpose(q).astype(BF16)
        if own is None:
            v = jnp.concatenate([nw[pl.ds(at, 16), :], nw[pl.ds(at + 16, 16), :]], 1)
            v = v * inside(wide // WIDE - 1, wide % WIDE - 1)
            vhl[wide] = jnp.concatenate(split2(v), 0)

    def near_pair(f, a, b, da, db):
        d = f - jnp.where(lane_row == 0, float(da), jnp.where(lane_row == 1, float(db), 0.0))
        sq = d * d
        m = sq[0:1] + sq[1:2] + sq[2:3]
        d = jnp.where(
            lane_row < 3,
            -2.0 * d,
            jnp.where(lane_row == 3, 1.0, jnp.where(lane_row == 4, m, 0.0)),
        )
        d1, d2, d3 = split3(d)
        p = jnp.concatenate([d1, d2, d3, d1, d2, d1], 0).astype(BF16)
        wide = (1 + a + da) * WIDE + 1 + b + db
        g = lax.rsqrt(dot(qt[wide], p))
        gh, gl = split2(g)
        v = vhl[wide]
        o = dot(v, gh)
        o = (o[:16] + o[16:]) + dot(v[:16], gl)
        return o * nmask[a * LC + b, 3 * (da + 1) + db + 1].astype(F32)

    def near_group(a, b, das):
        f = feat[a * LC + b]
        total = None
        for da in das:
            for db in (-1, 0, 1):
                term = near_pair(f, a, b, da, db)
                total = term if total is None else total + term
        return total

    def near_own(b):
        nacc[b] += near_group(0, b, (0, 1))
        nacc[LC + b] += near_group(1, b, (-1, 0))

    def near_outer(b):
        nacc[b] += near_group(0, b, (-1,))
        nacc[LC + b] += near_group(1, b, (1,))

    def weights():
        for n in range(3, 7):
            loads[late + n].wait()
        for w_ref, source in ((wf, coupling), (wt, topc)):

            @pl.loop(0, 8)
            def _(n):
                for m in range(2):
                    k = pl.ds(pl.multiple_of(n * (2 * RANK) + m * RANK, RANK), RANK)
                    w = jnp.concatenate(split2(source[k, :]), 0)
                    w_ref[n, :, m * 128 : (m + 1) * 128] = jnp.concatenate([w, w], 1)

    def own_features():
        @pl.loop(0, LR * LC // 4)
        def _(i):
            for t in (4 * i, 4 * i + 1, 4 * i + 2, 4 * i + 3):
                features((1 + t // LC) * WIDE + 1 + t % LC, t)

    def near_inner(low, high):
        @pl.loop(low, high)
        def _(b):
            near_own(b)

    def carried():
        @pl.loop(0, LR * LC // 2)
        def _(i):
            for t in (2 * i, 2 * i + 1):
                k = pl.ds(pl.multiple_of(t * RANK, RANK), RANK)
                thi, tlo = split2(jnp.transpose(transfer[k, :]))
                q = dot(jnp.concatenate([thi, tlo], 0), bh[k, :])
                q = (q[:RANK] + q[RANK:]) + dot(thi, bl[k, :])
                gp[t] = dot(jnp.concatenate(split2(q), 0), perm[t], NT).astype(BF16)

    def halo_features():
        done(nrecv, near_bytes)

        @pl.loop(0, WIDE // 2)
        def _(i):
            for c in (2 * i, 2 * i + 1):
                for r in (0, 3):
                    features(r * WIDE + c, None)

        for r in (1, 2):
            for c in (0, WIDE - 1):
                features(r * WIDE + c, None)

    def near_ends():
        @pl.loop(0, 2)
        def _(i):
            near_own(i * (LC - 1))

    def near_beyond(low, high):
        @pl.loop(low, high)
        def _(b):
            near_outer(b)

    def far_field():
        done(crecv, coef_bytes)

        @pl.loop(0, LC + 4)
        def _(c):
            for r in range(LR + 4):
                eh[r, c], el[r, c] = split2(spread(cw[r, c] * inside(r - 2, c - 2)))

        @pl.loop(0, LC)
        def _(b):
            for o, (da, db) in enumerate(far_offsets()):
                for a in range(LR):
                    on = fmask[a * LC + b, o].astype(F32)
                    on = jnp.full((16, 128), on, F32).astype(BF16)
                    lanes = slice((o % 2) * 128, (o % 2) * 128 + 128)
                    at = pl.multiple_of((a * LC + b) * 16, 16)
                    am[o // 2, pl.ds(at, 16), lanes] = eh[2 + a + da, 2 + b + db] * on
                    am[o // 2, pl.ds(at + 256, 16), lanes] = el[2 + a + da, 2 + b + db] * on

        far = dot(am[0], wf[0], NT)
        for o in range(1, 8):
            far = far + dot(am[o], wf[o], NT)
        far = far[:256] + far[256:]
        far = far + pltpu.roll(far, RANK, 1)
        fh, fl = split2(far)
        am[0, 0:256, 0:128] = fh
        am[0, 256:512, 0:128] = fl

    def base_result():
        @pl.loop(0, LR * LC // 4)
        def _(i):
            for t in (4 * i, 4 * i + 1, 4 * i + 2, 4 * i + 3):
                k = pl.ds(pl.multiple_of(t * RANK, RANK), RANK)
                at = pl.multiple_of(t * 16, 16)
                f_hi, f_lo = am[0, pl.ds(at, 16), 0:RANK], am[0, pl.ds(at + 256, 16), 0:RANK]
                q = dot(jnp.concatenate([f_hi, f_lo], 0), bh[k, :])
                q = (q[:16] + q[16:]) + dot(f_hi, bl[k, :])
                q = q + nacc[t] * (1.0 / 48.0)
                q = dot(jnp.concatenate(split2(q), 0), perm[t], NT)
                nacc[t] = q[:16] + q[16:]

    blocks = dict(
        w=weights, f=own_features, m=lambda: near_inner(1, LC // 2), n=lambda: near_inner(LC // 2, LC - 1), g=carried, h=halo_features, e=near_ends,
        a=lambda: near_beyond(0, LC // 2), b=lambda: near_beyond(LC // 2, LC), l=far_field, r=base_result,
    )
    ahead = me_z < AHEAD

    def work(slot):
        early, other = PLAN[slot]
        if early == other:
            for name in early:
                blocks[name]()
            return
        for names, which in ((early, ahead), (other, jnp.logical_not(ahead))):
            if names:

                @pl.when(which)
                def _():
                    for name in names:
                        blocks[name]()

    def added(first, others, count):
        terms = [first] + [others[i] for i in range(1, count)]
        while len(terms) > 1:
            terms = [sum(terms[i : i + 2][1:], terms[i]) for i in range(0, len(terms), 2)]
        return terms[0]

    work("enter")
    pl.semaphore_wait(barrier, (group - 1) + (ny - 1) + (nz - 1) + len(around))
    sent(copy_a, group)
    for copy in near_copies():
        copy.start()
    for copy in coef_copies():
        copy.start()
    work("a")
    done(arecv, member_bytes)
    mine_y[...] = added(send_a[me_g], recv_a, group)
    sent(copy_y, ny)
    work("y")
    done(yrecv, y_bytes)
    mine_z[...] = added(mine_y[...], recv_y, ny)
    sent(copy_z, nz)
    work("z")
    done(zrecv, z_bytes)
    recv_c[0] = added(mine_z[...], recv_z, nz)
    sent(copy_c, group)
    work("c")
    done(drecv, member_bytes)
    acc = None
    for pair in range(8):
        parts = []
        for d in (2 * pair, 2 * pair + 1):
            h = (owner - d + TOPN) % TOPN
            m = (me_g - h // slots + group) % group
            tile = recv_c[m, pl.ds(0, 8), :] if slots == 1 else recv_c[m, pl.ds(pl.multiple_of((h % slots) * 8, 8), 8), :]
            if d == 0:
                tile = jnp.zeros_like(tile)
            parts.append(spread(tile))
        hi, lo = split2(jnp.concatenate(parts, 1))
        term = dot(jnp.concatenate([hi, lo], 0), wt[pair], NT)
        acc = term if acc is None else acc + term
    acc = acc[:16] + acc[16:]
    acc = acc + pltpu.roll(acc, RANK, 1)
    hi, lo = split2(acc)
    zero = jnp.zeros_like(acc)
    dl = jnp.concatenate(
        [hi.astype(F32), jnp.where(low_lanes16, lo.astype(F32), zero)], 0
    ).astype(BF16)

    for t in range(LR * LC):
        q = dot(dl, gp[t])
        q = (q[:16] + q[16:]) + nacc[t]
        for h in range(2):
            vout[h, pl.ds(t, 16, stride=16), :] = q[:, h * 128 : (h + 1) * 128]

    stores = [pltpu.make_async_copy(vout.at[h], out.at[:, half[h]], io_sem.at[h]) for h in range(2)]
    for copy in stores:
        copy.start()

    done(asend, member_bytes)
    done(ysend, y_bytes)
    done(zsend, z_bytes)
    done(dsend, member_bytes)
    done(nsend, near_bytes)
    done(csend, coef_bytes)
    for copy in stores:
        copy.wait()


def on_device(
    dims,
    vectors,
    leaf_order,
    offsets,
    near_mask,
    far_mask,
    basis,
    transfer,
    coupling,
    top_coupling,
    cluster_owner,
):
    nx, nzl, ny, nzh, nc = dims
    group, nz = nx * nc, nzh * nzl
    slots = TOPN // group
    hbm = pl.BlockSpec(memory_space=pltpu.HBM)
    dma = pltpu.SemaphoreType.DMA
    result = pl.pallas_call(
        functools.partial(kernel, dims),
        out_shape=jax.ShapeDtypeStruct((RHS * LR * LC, LEAF), F32),
        in_specs=[hbm] * 10,
        out_specs=pl.BlockSpec(memory_space=pl.ANY),
        scratch_shapes=[
            pltpu.VMEM((2, 256, 128), F32),
            pltpu.VMEM((2, 256, 128), F32),
            pltpu.VMEM((LR * LC, LEAF), jnp.int32),
            pltpu.VMEM((3 * LR * LC, LEAF), F32),
            pltpu.VMEM((1024, LEAF), F32),
            pltpu.VMEM((1024, RANK), F32),
            pltpu.VMEM((1024, RANK), F32),
            pltpu.VMEM((1024, RANK), F32),
            pltpu.SMEM((LR * LC, 9), jnp.int32),
            pltpu.SMEM((LR * LC, 16), jnp.int32),
            pltpu.SMEM((1, 1), jnp.int32),
            dma((10 + CHUNKS,)),
            pltpu.VMEM((4 * WIDE * REC, 128), F32),
            pltpu.VMEM((LR + 4, LC + 4, 8, 128), F32),
            pltpu.VMEM((16, LEAF, LEAF), BF16),
            pltpu.VMEM((1024, LEAF), BF16),
            pltpu.VMEM((1024, LEAF), BF16),
            pltpu.VMEM((1024, RANK), BF16),
            pltpu.VMEM((1024, RANK), BF16),
            pltpu.VMEM((32, 1024), BF16),
            pltpu.VMEM((16, 8, LEAF), F32),
            pltpu.VMEM((4 * WIDE, LEAF, 48), BF16),
            pltpu.VMEM((4 * WIDE, 32, LEAF), BF16),
            pltpu.VMEM((8, 128, 256), BF16),
            pltpu.VMEM((8, 128, 256), BF16),
            pltpu.VMEM((16, 128, LEAF), BF16),
            pltpu.VMEM((16, 16, LEAF), F32),
            pltpu.VMEM((LR + 4, LC + 4, 16, 128), BF16),
            pltpu.VMEM((LR + 4, LC + 4, 16, 128), BF16),
            pltpu.VMEM((8, 512, 256), BF16),
            pltpu.VMEM((group, 8 * slots, 128), F32),
            pltpu.VMEM((group, 8 * slots, 128), F32),
            pltpu.VMEM((8 * slots, 128), F32),
            pltpu.VMEM((ny, 8 * slots, 128), F32),
            pltpu.VMEM((8 * slots, 128), F32),
            pltpu.VMEM((nz, 8 * slots, 128), F32),
            pltpu.VMEM((group, 8 * slots, 128), F32),
            *[dma(())] * 12,
        ],
        compiler_params=pltpu.CompilerParams(
            collective_id=0, has_side_effects=True, vmem_limit_bytes=67000000
        ),
        name="operator",
    )(
        vectors.reshape(RHS * LR * LC, LEAF),
        leaf_order.reshape(LR * LC, LEAF),
        offsets.reshape(3 * LR * LC, LEAF),
        near_mask.transpose(1, 2, 0).reshape(LR * LC, 9),
        far_mask.transpose(1, 2, 0).reshape(LR * LC, 16),
        basis.reshape(LR * LC * RANK, LEAF),
        transfer.reshape(LR * LC * RANK, RANK),
        coupling.reshape(16 * RANK, RANK),
        top_coupling.reshape(TOPN * RANK, RANK),
        cluster_owner,
    )
    return result.reshape(RHS, LR, LC, LEAF)


def solution(mesh, dims=(8, 2, 8, 4, 2)):
    in_specs = (
        P(None, "row", "col", None),
        P("row", "col", None),
        P(None, "row", "col", None),
        P(None, "row", "col"),
        P(None, "row", "col"),
        P("row", "col", None, None),
        P("row", "col", None, None),
        P(),
        P(),
        P("row", "col"),
    )
    out_specs = P(None, "row", "col", None)
    return jax.shard_map(
        functools.partial(on_device, dims),
        mesh=mesh,
        in_specs=in_specs,
        out_specs=out_specs,
        check_vma=False,
    )
```

```python
import functools

import jax
import jax.numpy as jnp
from jax import lax
from jax.experimental import pallas as pl
from jax.experimental.pallas import tpu as pltpu
from jax.sharding import PartitionSpec as P

F32, BF16 = jnp.float32, jnp.bfloat16
MESH = pl.DeviceIdType.MESH
RHS, LR, LC, LEAF, RANK, TOPN = 16, 2, 8, 256, 64, 16
WIDE = LC + 2
REC = 40
softening = 0.01

CHUNKS = 4
UNROLL = LR * LC // CHUNKS
AHEAD = 3
PLAN = dict(enter=("wfng", ""), a=("m", "wfg"), y=("h", "m"), z=("la", "hla"), c=("ebr", "nebr"))

NN = (((1,), (0,)), ((), ()))
NT = (((1,), (1,)), ((), ()))
TN = (((0,), (0,)), ((), ()))


def far_offsets():
    return [(i, j) for i in range(-2, 3) for j in range(-2, 3) if max(abs(i), abs(j)) == 2]


def dot(a, b, dims=NN):
    return lax.dot_general(a, b, dims, preferred_element_type=F32)


def split2(x):
    hi = x.astype(BF16)
    return hi, (x - hi.astype(F32)).astype(BF16)


def split3(x):
    a = x.astype(BF16).astype(F32)
    r = x - a
    b = r.astype(BF16).astype(F32)
    return a, b, r - b


def kernel(
    dims,
    vec,
    order_in,
    off_in,
    nmask_in,
    fmask_in,
    basis_in,
    transfer_in,
    coupling_in,
    topc_in,
    owner_in,
    out,
    vin,
    vout,
    order,
    off,
    basis,
    transfer,
    coupling,
    topc,
    nmask,
    fmask,
    owner_ref,
    io_sem,
    nw,
    cw,
    perm,
    bh,
    bl,
    th,
    tl,
    lead,
    feat,
    qt,
    vhl,
    wf,
    wt,
    gp,
    nacc,
    eh,
    el,
    am,
    send_a,
    recv_a,
    mine_y,
    recv_y,
    mine_z,
    recv_z,
    recv_c,
    nsend,
    nrecv,
    csend,
    crecv,
    asend,
    arecv,
    ysend,
    yrecv,
    zsend,
    zrecv,
    dsend,
    drecv,
):
    nx, nzl, ny, nzh, nc = dims
    rows_n, cols_n = nzh * nc, nx * nzl * ny
    group, nz = nx * nc, nzh * nzl
    row, col = lax.axis_index("row"), lax.axis_index("col")
    zh, core = row // nc, row % nc
    x, zl, y = col // (nzl * ny), (col // ny) % nzl, col % ny
    me_g, me_z = x * nc + core, zh * nzl + zl

    def member(i):
        return (zh * nc + i % nc, (i // nc) * (nzl * ny) + zl * ny + y)

    def along_y(i):
        return (row, x * (nzl * ny) + zl * ny + i)

    def along_z(i):
        return ((i // nzl) * nc + core, x * (nzl * ny) + (i % nzl) * ny + y)

    def beside(dr, dc):
        return ((row + dr + rows_n) % rows_n, (col + dc + cols_n) % cols_n)

    half = [slice(0, 128), slice(128, 256)]
    moves = [
        (order_in, order),
        (vec.at[:, half[0]], vin.at[0]),
        (vec.at[:, half[1]], vin.at[1]),
    ]
    part = LR * LC * RANK // CHUNKS
    moves += [(basis_in.at[pl.ds(n * part, part)], basis.at[pl.ds(n * part, part)]) for n in range(CHUNKS)]
    late = len(moves)
    moves += [
        (off_in, off),
        (transfer_in, transfer),
        (owner_in, owner_ref),
        (nmask_in, nmask),
        (fmask_in, fmask),
        (topc_in, topc),
        (coupling_in, coupling),
    ]
    loads = [pltpu.make_async_copy(a, b, io_sem.at[n]) for n, (a, b) in enumerate(moves)]
    for copy in loads:
        copy.start()

    around = [(i, j) for i in (-1, 0, 1) for j in (-1, 0, 1) if (i, j) != (0, 0)]
    barrier = pltpu.get_barrier_semaphore()

    def greet(device):
        pl.semaphore_signal(barrier, inc=1, device_id=device, device_id_type=MESH)

    @pl.loop(1, group)
    def _(i):
        greet(member((me_g + i) % group))

    @pl.loop(1, ny)
    def _(i):
        greet(along_y((y + i) % ny))

    @pl.loop(1, nz)
    def _(i):
        greet(along_z((me_z + i) % nz))

    for step in around:
        greet(beside(*step))

    nacc[...] = jnp.zeros_like(nacc)
    low_lanes = lax.broadcasted_iota(jnp.int32, (8, 128), 1) < RANK
    low_lanes16 = lax.broadcasted_iota(jnp.int32, (16, 128), 1) < RANK

    def spread(tile):
        return jnp.concatenate(
            [jnp.where(low_lanes, tile, 0.0), jnp.where(low_lanes, 0.0, tile)], 0
        )

    def rec_of(wide):
        return pl.multiple_of(wide * REC, 8)

    for n in range(3):
        loads[n].wait()
    lane_q = lax.broadcasted_iota(jnp.int32, (LEAF, LEAF), 0)

    def sort_leaf(t):
        hot = jnp.where(lane_q == order[pl.ds(t, 1), :], 1.0, 0.0).astype(BF16)
        perm[t] = hot
        v = jnp.concatenate(
            [vin[h, pl.ds(t, 16, stride=16), :] for h in range(2)], 1
        )
        parts = dot(jnp.concatenate(split2(v), 0), hot)
        wide = (1 + t // LC) * WIDE + 1 + t % LC
        at = rec_of(wide)
        for h in range(2):
            both = parts[:16, h * 128 : (h + 1) * 128] + parts[16:, h * 128 : (h + 1) * 128]
            nw[pl.ds(at + 16 * h, 16), :] = both
        sorted2 = parts.astype(BF16)
        vhl[wide] = sorted2
        k = pl.ds(pl.multiple_of(t * RANK, RANK), RANK)
        hi, lo = split2(basis[k, :])
        bh[k, :], bl[k, :] = hi, lo
        c4 = dot(sorted2, jnp.concatenate([hi, lo], 0), NT)
        c2 = c4[:16] + c4[16:]
        c = c2 + pltpu.roll(c2, RANK, 1)
        cw[2 + t // LC, 2 + t % LC] = jnp.where(low_lanes, c[:8], c[8:])
        return c

    @pl.loop(0, CHUNKS)
    def _(i):
        rows = pl.ds(pl.multiple_of(i * part, part), part)
        pltpu.make_async_copy(basis_in.at[rows], basis.at[rows], io_sem.at[3 + i]).wait()
        cs = [sort_leaf(UNROLL * i + n) for n in range(UNROLL)]
        for n in range(0, UNROLL, 2):
            hi, lo = split2(jnp.where(low_lanes16, cs[n], cs[n + 1]))
            at = pl.multiple_of(i * (UNROLL * RANK) + n * RANK, 128)
            lead[:, pl.ds(at, 128)] = jnp.concatenate([hi, lo], 0)

    loads[late + 1].wait()
    loads[late + 2].wait()
    owner = owner_ref[0, 0]
    th[...], tl[...] = split2(transfer[...])
    cl = dot(lead[...], th[...])
    cl = (cl[:16] + cl[16:]) + dot(lead[0:16, :], tl[...])
    packed = jnp.concatenate([cl[:8], cl[8:]], 1)
    slots = TOPN // group
    for g in range(group):
        for s in range(slots):
            send_a[g, 8 * s : 8 * s + 8, :] = jnp.where(owner == g * slots + s, packed, 0.0)

    loads[late].wait()
    base = lax.broadcasted_iota(jnp.int32, (LR * LC, LEAF), 0)
    row_first = (row * LR + base // LC).astype(F32)
    col_first = (col * LC + base % LC).astype(F32)
    px = ((row_first + off[0:16, :]) - row_first) - 0.5
    py = ((col_first + off[16:32, :]) - col_first) - 0.5
    pz = 0.25 * off[32:48, :] - 0.125
    pn = (px * px + py * py + pz * pz) + softening
    for r in range(LR):
        first = ((1 + r) * WIDE + 1) * REC + 32
        for h in range(2):
            for c, value in enumerate((px, py, pz, pn)):
                nw[pl.ds(first + 4 * h + c, LC, stride=REC), :] = value[
                    r * LC : (r + 1) * LC, h * 128 : (h + 1) * 128
                ]

    def near_copies():
        found = []
        for n, (dr, dc) in enumerate(around):
            rs = {-1: [1], 0: [1, 2], 1: [2]}[dr]
            c0, count = {-1: (1, 1), 0: (1, LC), 1: (LC, 1)}[dc]
            for r in rs:
                r_to = r - 2 * dr
                c_to = c0 - LC * dc
                found.append((
                    nw.at[pl.ds((r * WIDE + c0) * REC, count * REC)],
                    nw.at[pl.ds((r_to * WIDE + c_to) * REC, count * REC)],
                    (dr, dc),
                ))
        return [
            pltpu.make_async_remote_copy(
                a, b, nsend, nrecv, device_id=beside(*s), device_id_type=MESH
            )
            for n, (a, b, s) in enumerate(found)
        ]

    def coef_copies():
        found = []
        for dr, dc in around:
            c0, count = {-1: (2, 2), 0: (2, LC), 1: (LC, 2)}[dc]
            r_to, c_to = 2 - 2 * dr, c0 - LC * dc
            found.append((
                cw.at[2:4, c0 : c0 + count],
                cw.at[r_to : r_to + 2, c_to : c_to + count],
                (dr, dc),
            ))
        return [
            pltpu.make_async_remote_copy(
                a, b, csend, crecv, device_id=beside(*s), device_id_type=MESH
            )
            for n, (a, b, s) in enumerate(found)
        ]

    def copy_a(i):
        to = (me_g + i) % group
        return pltpu.make_async_remote_copy(
            send_a.at[to], recv_a.at[i], asend, arecv,
            device_id=member(to), device_id_type=MESH,
        )

    def copy_y(i):
        return pltpu.make_async_remote_copy(
            mine_y, recv_y.at[i], ysend, yrecv,
            device_id=along_y((y + i) % ny), device_id_type=MESH,
        )

    def copy_z(i):
        return pltpu.make_async_remote_copy(
            mine_z, recv_z.at[i], zsend, zrecv,
            device_id=along_z((me_z + i) % nz), device_id_type=MESH,
        )

    def copy_c(i):
        return pltpu.make_async_remote_copy(
            recv_c.at[0], recv_c.at[i], dsend, drecv,
            device_id=member((me_g + i) % group), device_id_type=MESH,
        )

    def sent(copy, count):
        for i in sorted(range(1, count), key=lambda i: abs(2 * i - count)):
            copy(i).start()

    def done(sem, ref):
        pltpu.make_async_copy(ref, ref, sem).wait()

    near_bytes = nw.at[pl.ds(0, (4 * WIDE - LR * LC) * REC)]
    coef_bytes = nw.at[pl.ds(0, ((LR + 4) * (LC + 4) - LR * LC) * 8)]
    member_bytes = recv_a.at[pl.ds(1, group - 1)]
    y_bytes = recv_y.at[pl.ds(1, ny - 1)]
    z_bytes = recv_z.at[pl.ds(1, nz - 1)]

    lane_row = lax.broadcasted_iota(jnp.int32, (8, LEAF), 0)

    def inside(r, c):
        r, c = row * LR + r, col * LC + c
        ok = (r >= 0) & (r < rows_n * LR) & (c >= 0) & (c < cols_n * LC)
        return jnp.where(ok, 1.0, 0.0)

    def features(wide, own):
        at = rec_of(wide)
        tile = nw[pl.ds(at + 32, 8), :]
        f = jnp.concatenate([tile, pltpu.roll(tile, 4, 0)], 1)
        f = jnp.where(lane_row < 4, f, jnp.where(lane_row == 4, 1.0, 0.0))
        if own is not None:
            feat[own] = f
        a, b, c = split3(f)
        q = jnp.concatenate([a, a, a, b, b, c], 0)
        qt[wide] = jnp.transpose(q).astype(BF16)
        if own is None:
            v = jnp.concatenate([nw[pl.ds(at, 16), :], nw[pl.ds(at + 16, 16), :]], 1)
            v = v * inside(wide // WIDE - 1, wide % WIDE - 1)
            vhl[wide] = jnp.concatenate(split2(v), 0)

    def near_pair(f, a, b, da, db):
        d = f - jnp.where(lane_row == 0, float(da), jnp.where(lane_row == 1, float(db), 0.0))
        sq = d * d
        m = sq[0:1] + sq[1:2] + sq[2:3]
        d = jnp.where(
            lane_row < 3,
            -2.0 * d,
            jnp.where(lane_row == 3, 1.0, jnp.where(lane_row == 4, m, 0.0)),
        )
        d1, d2, d3 = split3(d)
        p = jnp.concatenate([d1, d2, d3, d1, d2, d1], 0).astype(BF16)
        wide = (1 + a + da) * WIDE + 1 + b + db
        g = lax.rsqrt(dot(qt[wide], p))
        gh, gl = split2(g)
        v = vhl[wide]
        o = dot(v, gh)
        o = (o[:16] + o[16:]) + dot(v[:16], gl)
        return o * nmask[a * LC + b, 3 * (da + 1) + db + 1].astype(F32)

    def near_group(a, b, das):
        f = feat[a * LC + b]
        total = None
        for da in das:
            for db in (-1, 0, 1):
                term = near_pair(f, a, b, da, db)
                total = term if total is None else total + term
        return total

    def near_own(b):
        nacc[b] += near_group(0, b, (0, 1))
        nacc[LC + b] += near_group(1, b, (-1, 0))

    def near_outer(b):
        nacc[b] += near_group(0, b, (-1,))
        nacc[LC + b] += near_group(1, b, (1,))

    def weights():
        for n in range(3, 7):
            loads[late + n].wait()
        for w_ref, source in ((wf, coupling), (wt, topc)):

            @pl.loop(0, 8)
            def _(n):
                for m in range(2):
                    k = pl.ds(pl.multiple_of(n * (2 * RANK) + m * RANK, RANK), RANK)
                    w = jnp.concatenate(split2(source[k, :]), 0)
                    w_ref[n, :, m * 128 : (m + 1) * 128] = jnp.concatenate([w, w], 1)

    def own_features():
        @pl.loop(0, LR * LC // 4)
        def _(i):
            for t in (4 * i, 4 * i + 1, 4 * i + 2, 4 * i + 3):
                features((1 + t // LC) * WIDE + 1 + t % LC, t)

    def near_inner(low, high):
        @pl.loop(low, high)
        def _(b):
            near_own(b)

    def carried():
        @pl.loop(0, LR * LC // 2)
        def _(i):
            for t in (2 * i, 2 * i + 1):
                k = pl.ds(pl.multiple_of(t * RANK, RANK), RANK)
                thi, tlo = split2(jnp.transpose(transfer[k, :]))
                q = dot(jnp.concatenate([thi, tlo], 0), bh[k, :])
                q = (q[:RANK] + q[RANK:]) + dot(thi, bl[k, :])
                gp[t] = dot(jnp.concatenate(split2(q), 0), perm[t], NT).astype(BF16)

    def halo_features():
        done(nrecv, near_bytes)

        @pl.loop(0, WIDE // 2)
        def _(i):
            for c in (2 * i, 2 * i + 1):
                for r in (0, 3):
                    features(r * WIDE + c, None)

        for r in (1, 2):
            for c in (0, WIDE - 1):
                features(r * WIDE + c, None)

    def near_ends():
        @pl.loop(0, 2)
        def _(i):
            near_own(i * (LC - 1))

    def near_beyond(low, high):
        @pl.loop(low, high)
        def _(b):
            near_outer(b)

    def far_field():
        done(crecv, coef_bytes)

        @pl.loop(0, LC + 4)
        def _(c):
            for r in range(LR + 4):
                eh[r, c], el[r, c] = split2(spread(cw[r, c] * inside(r - 2, c - 2)))

        @pl.loop(0, LC)
        def _(b):
            for o, (da, db) in enumerate(far_offsets()):
                for a in range(LR):
                    on = fmask[a * LC + b, o].astype(F32)
                    on = jnp.full((16, 128), on, F32).astype(BF16)
                    lanes = slice((o % 2) * 128, (o % 2) * 128 + 128)
                    at = pl.multiple_of((a * LC + b) * 16, 16)
                    am[o // 2, pl.ds(at, 16), lanes] = eh[2 + a + da, 2 + b + db] * on
                    am[o // 2, pl.ds(at + 256, 16), lanes] = el[2 + a + da, 2 + b + db] * on

        far = dot(am[0], wf[0], NT)
        for o in range(1, 8):
            far = far + dot(am[o], wf[o], NT)
        far = far[:256] + far[256:]
        far = far + pltpu.roll(far, RANK, 1)
        fh, fl = split2(far)
        am[0, 0:256, 0:128] = fh
        am[0, 256:512, 0:128] = fl

    def base_result():
        @pl.loop(0, LR * LC // 4)
        def _(i):
            for t in (4 * i, 4 * i + 1, 4 * i + 2, 4 * i + 3):
                k = pl.ds(pl.multiple_of(t * RANK, RANK), RANK)
                at = pl.multiple_of(t * 16, 16)
                f_hi, f_lo = am[0, pl.ds(at, 16), 0:RANK], am[0, pl.ds(at + 256, 16), 0:RANK]
                q = dot(jnp.concatenate([f_hi, f_lo], 0), bh[k, :])
                q = (q[:16] + q[16:]) + dot(f_hi, bl[k, :])
                q = q + nacc[t] * (1.0 / 48.0)
                q = dot(jnp.concatenate(split2(q), 0), perm[t], NT)
                nacc[t] = q[:16] + q[16:]

    blocks = dict(
        w=weights, f=own_features, m=lambda: near_inner(1, LC // 2), n=lambda: near_inner(LC // 2, LC - 1), g=carried, h=halo_features, e=near_ends,
        a=lambda: near_beyond(0, LC // 2), b=lambda: near_beyond(LC // 2, LC), l=far_field, r=base_result,
    )
    ahead = me_z < AHEAD

    def work(slot):
        early, other = PLAN[slot]
        if early == other:
            for name in early:
                blocks[name]()
            return
        for names, which in ((early, ahead), (other, jnp.logical_not(ahead))):
            if names:

                @pl.when(which)
                def _():
                    for name in names:
                        blocks[name]()

    def added(first, others, count):
        terms = [first] + [others[i] for i in range(1, count)]
        while len(terms) > 1:
            terms = [sum(terms[i : i + 2][1:], terms[i]) for i in range(0, len(terms), 2)]
        return terms[0]

    work("enter")
    pl.semaphore_wait(barrier, (group - 1) + (ny - 1) + (nz - 1) + len(around))
    sent(copy_a, group)
    for copy in near_copies():
        copy.start()
    for copy in coef_copies():
        copy.start()
    work("a")
    done(arecv, member_bytes)
    mine_y[...] = added(send_a[me_g], recv_a, group)
    sent(copy_y, ny)
    work("y")
    done(yrecv, y_bytes)
    mine_z[...] = added(mine_y[...], recv_y, ny)
    sent(copy_z, nz)
    work("z")
    done(zrecv, z_bytes)
    recv_c[0] = added(mine_z[...], recv_z, nz)
    sent(copy_c, group)
    work("c")
    done(drecv, member_bytes)
    acc = None
    for pair in range(8):
        parts = []
        for d in (2 * pair, 2 * pair + 1):
            h = (owner - d + TOPN) % TOPN
            m = (me_g - h // slots + group) % group
            tile = recv_c[m, pl.ds(0, 8), :] if slots == 1 else recv_c[m, pl.ds(pl.multiple_of((h % slots) * 8, 8), 8), :]
            if d == 0:
                tile = jnp.zeros_like(tile)
            parts.append(spread(tile))
        hi, lo = split2(jnp.concatenate(parts, 1))
        term = dot(jnp.concatenate([hi, lo], 0), wt[pair], NT)
        acc = term if acc is None else acc + term
    acc = acc[:16] + acc[16:]
    acc = acc + pltpu.roll(acc, RANK, 1)
    hi, lo = split2(acc)
    zero = jnp.zeros_like(acc)
    dl = jnp.concatenate(
        [hi.astype(F32), jnp.where(low_lanes16, lo.astype(F32), zero)], 0
    ).astype(BF16)

    for t in range(LR * LC):
        q = dot(dl, gp[t])
        q = (q[:16] + q[16:]) + nacc[t]
        for h in range(2):
            vout[h, pl.ds(t, 16, stride=16), :] = q[:, h * 128 : (h + 1) * 128]

    stores = [pltpu.make_async_copy(vout.at[h], out.at[:, half[h]], io_sem.at[h]) for h in range(2)]
    for copy in stores:
        copy.start()

    done(asend, member_bytes)
    done(ysend, y_bytes)
    done(zsend, z_bytes)
    done(dsend, member_bytes)
    done(nsend, near_bytes)
    done(csend, coef_bytes)
    for copy in stores:
        copy.wait()


def on_device(
    dims,
    vectors,
    leaf_order,
    offsets,
    near_mask,
    far_mask,
    basis,
    transfer,
    coupling,
    top_coupling,
    cluster_owner,
):
    nx, nzl, ny, nzh, nc = dims
    group, nz = nx * nc, nzh * nzl
    slots = TOPN // group
    hbm = pl.BlockSpec(memory_space=pltpu.HBM)
    dma = pltpu.SemaphoreType.DMA
    result = pl.pallas_call(
        functools.partial(kernel, dims),
        out_shape=jax.ShapeDtypeStruct((RHS * LR * LC, LEAF), F32),
        in_specs=[hbm] * 10,
        out_specs=pl.BlockSpec(memory_space=pl.ANY),
        scratch_shapes=[
            pltpu.VMEM((2, 256, 128), F32),
            pltpu.VMEM((2, 256, 128), F32),
            pltpu.VMEM((LR * LC, LEAF), jnp.int32),
            pltpu.VMEM((3 * LR * LC, LEAF), F32),
            pltpu.VMEM((1024, LEAF), F32),
            pltpu.VMEM((1024, RANK), F32),
            pltpu.VMEM((1024, RANK), F32),
            pltpu.VMEM((1024, RANK), F32),
            pltpu.SMEM((LR * LC, 9), jnp.int32),
            pltpu.SMEM((LR * LC, 16), jnp.int32),
            pltpu.SMEM((1, 1), jnp.int32),
            dma((10 + CHUNKS,)),
            pltpu.VMEM((4 * WIDE * REC, 128), F32),
            pltpu.VMEM((LR + 4, LC + 4, 8, 128), F32),
            pltpu.VMEM((16, LEAF, LEAF), BF16),
            pltpu.VMEM((1024, LEAF), BF16),
            pltpu.VMEM((1024, LEAF), BF16),
            pltpu.VMEM((1024, RANK), BF16),
            pltpu.VMEM((1024, RANK), BF16),
            pltpu.VMEM((32, 1024), BF16),
            pltpu.VMEM((16, 8, LEAF), F32),
            pltpu.VMEM((4 * WIDE, LEAF, 48), BF16),
            pltpu.VMEM((4 * WIDE, 32, LEAF), BF16),
            pltpu.VMEM((8, 128, 256), BF16),
            pltpu.VMEM((8, 128, 256), BF16),
            pltpu.VMEM((16, 128, LEAF), BF16),
            pltpu.VMEM((16, 16, LEAF), F32),
            pltpu.VMEM((LR + 4, LC + 4, 16, 128), BF16),
            pltpu.VMEM((LR + 4, LC + 4, 16, 128), BF16),
            pltpu.VMEM((8, 512, 256), BF16),
            pltpu.VMEM((group, 8 * slots, 128), F32),
            pltpu.VMEM((group, 8 * slots, 128), F32),
            pltpu.VMEM((8 * slots, 128), F32),
            pltpu.VMEM((ny, 8 * slots, 128), F32),
            pltpu.VMEM((8 * slots, 128), F32),
            pltpu.VMEM((nz, 8 * slots, 128), F32),
            pltpu.VMEM((group, 8 * slots, 128), F32),
            *[dma(())] * 12,
        ],
        compiler_params=pltpu.CompilerParams(
            collective_id=0, has_side_effects=True, vmem_limit_bytes=67000000
        ),
        name="operator",
    )(
        vectors.reshape(RHS * LR * LC, LEAF),
        leaf_order.reshape(LR * LC, LEAF),
        offsets.reshape(3 * LR * LC, LEAF),
        near_mask.transpose(1, 2, 0).reshape(LR * LC, 9),
        far_mask.transpose(1, 2, 0).reshape(LR * LC, 16),
        basis.reshape(LR * LC * RANK, LEAF),
        transfer.reshape(LR * LC * RANK, RANK),
        coupling.reshape(16 * RANK, RANK),
        top_coupling.reshape(TOPN * RANK, RANK),
        cluster_owner,
    )
    return result.reshape(RHS, LR, LC, LEAF)


def solution(mesh, dims=(8, 2, 8, 4, 2)):
    in_specs = (
        P(None, "row", "col", None),
        P("row", "col", None),
        P(None, "row", "col", None),
        P(None, "row", "col"),
        P(None, "row", "col"),
        P("row", "col", None, None),
        P("row", "col", None, None),
        P(),
        P(),
        P("row", "col"),
    )
    out_specs = P(None, "row", "col", None)
    return jax.shard_map(
        functools.partial(on_device, dims),
        mesh=mesh,
        in_specs=in_specs,
        out_specs=out_specs,
        check_vma=False,
    )
```
